512 devices in a mesh: dp: 64 (over x, z_hi, y), rollout: 8 (over z_lo, core).
Axes of the slice: x: 4, y: 4, z: 16 (z_hi: 4, z_lo: 4; z = z_hi * 4 + z_lo), core: 2. Of those that a mesh axis runs over, the one named last changes fastest.
Arguments:
- layer_inputs: bfloat16 [8, 49152, 512], P('rollout', 'dp'), may hold values from -6 to 6
- cotangent: bfloat16 [8, 49152, 2048], P('rollout', 'dp'), may hold values from -0.02734375 to 0.02734375
- master: float32 [8, 512, 2048], P('rollout', 'dp'), may hold values from -6 to 6
- first_moment: float32 [8, 512, 2048], P('rollout', 'dp'), may hold values from -6 to 6
- second_moment: float32 [8, 512, 2048], P('rollout', 'dp'), may hold values from 0.01 to 4
- step_count: int32 [8], P('rollout'), may hold values from 1 to 1999
- bucket_owner: int32 [8], replicated, may hold values from 0 to 7, each once
Outputs:
- new_master: float32 [8, 512, 2048], P('rollout', 'dp')
- new_first: float32 [8, 512, 2048], P('rollout', 'dp')
- new_second: float32 [8, 512, 2048], P('rollout', 'dp')
- published: bfloat16 [8, 512, 2048], P(None, 'dp')
The draws below stay inside these ranges and needn't reach their ends.
Inputs may be any that keep to these rules, and one draw needn't show every extreme that they name: `bucket_owner`: each group is named once.
All inputs are finite; a program needn't handle non-finite values.
Results may differ from the reference program's by a relative error of at most 0.001.
Values may be sent and summed in bfloat16 or wider, within the bound.
A program may use at most 64 MiB of HBM per device.

```python
import math
import jax
import jax.numpy as jnp
from jax import lax

FF = 2048
TOK_DEV = 768
ROWS = 512
TOKENS = 49152
N_DP = 64
N_ROLLOUT = 8


def set_ends(values, stream_key, least, top_value):
    extent = values.shape
    spot = [jax.random.randint(jax.random.fold_in(stream_key, axis), (), 0, extent[axis]) for axis in range(len(extent))]
    values = values.at[tuple(spot)].set(least)
    longest = extent.index(max(extent))
    spot[longest] = (spot[longest] + 1) % extent[longest]
    return values.at[tuple(spot)].set(top_value)


def level_of(key, shape, split, low, largest):
    def one(position, shards_of):
        heights = jax.random.uniform(jax.random.fold_in(jax.random.fold_in(key, 6), position), (shards_of,), jnp.float32, low / len(split), largest / len(split))
        return jnp.repeat(jnp.exp(heights), shape[position] // shards_of).reshape((-1,) + (1,) * (len(shape) - position - 1))

    gain = one(*split[0])
    for cut in split[1:]:
        gain = gain * one(*cut)
    return gain


def normal_values(own_key, dims, scale, limit, split=(), dtype=jnp.bfloat16):
    gain = level_of(own_key, dims, split, -0.22, 0.18) if split else 1.0
    drawn = jax.random.normal(own_key, dims, jnp.float32) * scale * gain
    return jnp.minimum(jnp.maximum(drawn, -limit), limit).astype(dtype)


def setup_inputs(seed: int = 0) -> dict:
    keys = jax.random.split(jax.random.key(seed), 8)
    return {
        "layer_inputs": normal_values(keys[0], (N_ROLLOUT, TOKENS, ROWS), 1.0, 6.0, ((0, 8), (1, 64))),
        "cotangent": normal_values(keys[1], (N_ROLLOUT, TOKENS, FF), TOKENS ** -0.5, 0.02734375, ((0, 8), (1, 64))),
        "master": normal_values(keys[2], (N_ROLLOUT, ROWS, FF), 1.0, 6.0, ((0, 8), (1, 64)), jnp.float32),
        "first_moment": normal_values(keys[3], (N_ROLLOUT, ROWS, FF), 1.0, 6.0, ((0, 8), (1, 64)), jnp.float32),
        "second_moment": jnp.clip(jnp.exp(math.log(4.0) - 5.9914646 * jax.random.uniform(keys[4], (N_ROLLOUT, ROWS, FF), jnp.float32) ** level_of(keys[4], (N_ROLLOUT, ROWS, FF), ((0, 8), (1, 64)), -0.2, 0.2)), 0.01, 4.0),
        "step_count": set_ends(jax.random.randint(keys[5], (N_ROLLOUT,), 1, 2000), jax.random.fold_in(keys[5], 1), 1, 1999).astype(jnp.int32),
        "bucket_owner": jax.random.permutation(keys[6], N_ROLLOUT).astype(jnp.int32),
    }


def group_grad(pair):
    left, right = pair
    left = left.reshape(N_DP, TOK_DEV, ROWS)
    right = right.reshape(N_DP, TOK_DEV, FF)

    def add_shard(total, piece):
        first, second = piece
        term = lax.dot_general(first.astype(jnp.float32), second.astype(jnp.float32), (((0,), (0,)), ((), ())), precision=lax.Precision.HIGHEST)
        rounded = lax.optimization_barrier(term.astype(jnp.bfloat16)).astype(jnp.float32)
        return (total + rounded, None)
    total, unused = lax.scan(add_shard, jnp.zeros((ROWS, FF), jnp.float32), (left, right))
    return total

def reference(layer_inputs, cotangent, master, first_moment, second_moment, step_count, bucket_owner):
    grad = lax.map(group_grad, (layer_inputs, cotangent))
    new_first = 0.9 * first_moment + 0.1 * grad
    new_second = 0.999 * second_moment + 0.001 * grad * grad
    counts = (step_count + 1).astype(jnp.float32)[:, None, None]
    corr_one = 1.0 - jnp.power(jnp.float32(0.9), counts)
    corr_two = 1.0 - jnp.power(jnp.float32(0.999), counts)
    update = new_first / corr_one / (jnp.sqrt(new_second / corr_two) + 1e-08) + 0.1 * master
    new_master = master - 0.02 * update
    published = jnp.take(new_master.astype(jnp.bfloat16), bucket_owner.astype(jnp.int32), axis=0)
    return (new_master, new_first, new_second, published)
```

```python
import functools
import math

import jax
import jax.numpy as jnp
from jax import lax
from jax.experimental import pallas as pl
from jax.experimental.pallas import tpu as pltpu
from jax.sharding import Mesh
from jax.sharding import PartitionSpec as P

MESH = pl.DeviceIdType.MESH
AXES = ("x", "zh", "y", "zl", "core")
DP = ("x", "zh", "y")
GROUP = ("zl", "core")
CHUNKS = 8
WIDE = 128
F32 = jnp.float32
BF16 = jnp.bfloat16


def order_of_work():
    events = []
    for k in range(CHUNKS):
        events.append((0.4 * k, 0, k))
        start = 2.5 + 1.3 * k
        for phase, lag in ((1, 0.0), (2, 2.5), (3, 4.5), (4, 6.5), (5, 10.5), (6, 14.5), (7, 18.5)):
            events.append((start + lag, phase, k))
    return [(phase, k) for _, phase, k in sorted(events)]


def kernel(
    x_hbm, ct_hbm, master_hbm, first_hbm, second_hbm, step_hbm, owner_hbm,
    master_out, first_out, second_out, pub_out,
    x_v, xt_v, ct_v, state_v, step_s, owner_s,
    w1, w2, w3, rx1, rx2, rx3, fw1, fw2, fw3, *rest,
):
    gathered = rest[:CHUNKS]
    in_sem, ct_sem, send1, recv1, send2, recv2, send3, recv3, psend, precv = rest[CHUNKS:]
    x, zh, y = (lax.axis_index(a) for a in DP)
    zl, core = (lax.axis_index(a) for a in GROUP)
    rank = zl * 2 + core

    barrier = pltpu.get_barrier_semaphore()
    near = [{a: lax.rem(i + d, 4)} for a, i in (("x", x), ("y", y), ("zh", zh)) for d in (1, 3)]
    peers = []
    for d in range(1, 8):
        other = lax.rem(rank + d, 8)
        peers.append({"zl": other // 2, "core": lax.rem(other, 2)})
    for device in near + peers:
        pl.semaphore_signal(barrier, inc=1, device_id=device, device_id_type=MESH)

    loads = [pltpu.make_async_copy(x_hbm.at[0], x_v, in_sem.at[0])]
    columns = []
    for k in range(CHUNKS):
        for h in range(2):
            columns.append(
                pltpu.make_async_copy(
                    ct_hbm.at[0, :, pl.ds(h * CHUNKS * WIDE + k * WIDE, WIDE)],
                    ct_v.at[k, :, pl.ds(h * WIDE, WIDE)],
                    ct_sem.at[k, h],
                )
            )
    for i, ref in enumerate((master_hbm, first_hbm, second_hbm)):
        loads.append(pltpu.make_async_copy(ref.at[0], state_v.at[i], in_sem.at[1 + i]))
    loads.append(pltpu.make_async_copy(step_hbm, step_s, in_sem.at[4]))
    loads.append(pltpu.make_async_copy(owner_hbm, owner_s, in_sem.at[5]))
    loads[0].start()
    for copy in columns + loads[1:]:
        copy.start()

    sources = (w1, w2, w3)
    landing = (rx1, rx2, rx3)
    relayed = (fw1, fw2, fw3)
    send_sems = (send1, send2, send3)
    recv_sems = (recv1, recv2, recv3)

    def place(stage, k):
        axis = "zh" if stage == 2 else ("x", "y")[(k + stage) % 2]
        return axis, {"x": x, "y": y, "zh": zh}[axis]

    def parts(stage, k):
        if stage == 0:
            return ((pl.ds(0, 2), 1), (pl.ds(2, 2), -1))
        if stage == 1:
            return ((pl.ds(0, 2), 1), (pl.ds(2, 2), -1))
        return ((pl.ds(0, 16), 1 if (k // 2) % 2 == 0 else -1),)

    def piece(stage, k, position, cut):
        return sources[stage].at[k, position, cut]

    def remote(stage, k, part, kind, src, axis, target):
        slot = part * 3 + kind
        return functools.partial(
            pltpu.make_async_remote_copy,
            src_ref=src,
            dst_ref=landing[stage].at[k, slot],
            send_sem=send_sems[stage].at[k, slot],
            recv_sem=recv_sems[stage].at[k, slot],
            device_id={axis: target},
            device_id_type=MESH,
        )

    def copies(stage, k):
        axis, pos = place(stage, k)
        found = []
        for part, (cut, way) in enumerate(parts(stage, k)):
            ahead = lax.rem(pos + 4 + way, 4)
            behind = lax.rem(pos + 4 - way, 4)
            far = lax.rem(pos + 2, 4)
            found.append((
                remote(stage, k, part, 0, piece(stage, k, far, cut), axis, ahead),
                remote(stage, k, part, 1, piece(stage, k, behind, cut), axis, behind),
                remote(stage, k, part, 2, relayed[stage].at[k, part], axis, ahead),
                ahead, pos, cut,
            ))
        return found

    def begin(stage, k):
        found = copies(stage, k)
        for c in found:
            c[0]().start()
        for c in found:
            c[1]().start()

    def relay(stage, k):
        for part, c in enumerate(copies(stage, k)):
            c[0]().wait_recv()
            mine = sources[stage][k, c[3], c[5]].astype(F32)
            total = mine + landing[stage][k, part * 3].astype(F32)
            relayed[stage][k, part] = total.astype(BF16)
            c[2]().start()

    def finish(stage, k):
        sums = []
        for part, c in enumerate(copies(stage, k)):
            c[1]().wait_recv()
            c[2]().wait_recv()
            mine = sources[stage][k, c[4], c[5]].astype(F32)
            sums.append(
                mine
                + landing[stage][k, part * 3 + 1].astype(F32)
                + landing[stage][k, part * 3 + 2].astype(F32)
            )
        return sums

    def product(k):
        for h in range(2):
            columns[2 * k + h].wait()
        res = lax.dot_general(
            xt_v[...], ct_v[k], (((1,), (0,)), ((), ())), preferred_element_type=F32
        )
        res = res.reshape(64, 8, 2 * WIDE)
        res = jnp.concatenate([res[:, :, :WIDE], res[:, :, WIDE:]], axis=1).astype(BF16)
        res = res.reshape(4, 4, 4, 16, WIDE)
        for i in range(4):
            for j in range(4):
                if k % 2 == 0:
                    w1[k, i, j] = res[i, :, j]
                else:
                    w1[k, j, i] = res[i, :, j]

    def publish(k):
        found = []
        for d, device in enumerate(peers):
            found.append(
                pltpu.make_async_remote_copy(
                    src_ref=gathered[k].at[rank],
                    dst_ref=gathered[k].at[rank],
                    send_sem=psend.at[k, d],
                    recv_sem=precv.at[k, d],
                    device_id=device,
                    device_id_type=MESH,
                )
            )
        return found

    def update(k, grad):
        t = (step_s[0] + 1).astype(F32)
        steps = jnp.full((8, WIDE), t, F32)
        corr_one = 1.0 - jnp.exp(steps * math.log(0.9))
        corr_two = 1.0 - jnp.exp(steps * math.log(0.999))
        news = []
        for h in range(2):
            cut = pl.ds(h * CHUNKS * WIDE + k * WIDE, WIDE)
            g = grad[8 * h : 8 * h + 8]
            old = state_v[0, :, cut]
            new_first = 0.9 * state_v[1, :, cut] + 0.1 * g
            new_second = 0.999 * state_v[2, :, cut] + 0.001 * g * g
            step = new_first / corr_one / (jnp.sqrt(new_second / corr_two) + 1e-08) + 0.1 * old
            new_master = old - 0.02 * step
            master_out[0, :, cut] = new_master
            first_out[0, :, cut] = new_first
            second_out[0, :, cut] = new_second
            news.append(new_master)
        gathered[k][rank] = jnp.concatenate(news, axis=0).astype(BF16)

    def run(phase, k):
        if phase == 0:
            product(k)
            if k == 0:
                pl.semaphore_wait(barrier, len(near) + len(peers))
            begin(0, k)
        elif phase == 1:
            relay(0, k)
        elif phase == 2:
            low, high = finish(0, k)
            w2[k, 0:2] = low.astype(BF16)
            w2[k, 2:4] = high.astype(BF16)
            begin(1, k)
        elif phase == 3:
            relay(1, k)
        elif phase == 4:
            low, high = finish(1, k)
            w3[k, 0:2] = low.astype(BF16)
            w3[k, 2:4] = high.astype(BF16)
            begin(2, k)
        elif phase == 5:
            relay(2, k)
        elif phase == 6:
            (grad,) = finish(2, k)
            update(k, grad)
            for copy in publish(k):
                copy.start()
        else:
            for copy in publish(k):
                copy.wait_recv()
            for b in range(8):
                block = gathered[k][owner_s[b]].astype(F32)
                for h in range(2):
                    cut = pl.ds(h * CHUNKS * WIDE + k * WIDE, WIDE)
                    pub_out[b, :, cut] = block[8 * h : 8 * h + 8].astype(BF16)

    loads[0].wait()
    xt_v[...] = x_v[...].T
    state_ready = False
    for phase, k in order_of_work():
        if phase == 6 and not state_ready:
            for copy in loads[1:]:
                copy.wait()
            state_ready = True
        run(phase, k)

    for k in range(CHUNKS):
        for stage in range(3):
            for c in copies(stage, k):
                for copy in c[:3]:
                    copy().wait_send()
        for copy in publish(k):
            copy.wait_send()


def per_device(layer_inputs, cotangent, master, first_moment, second_moment, step_count, owner):
    tokens, rows = layer_inputs.shape[1:]
    wide = cotangent.shape[2]
    any_space = pl.BlockSpec(memory_space=pl.ANY)
    vmem = pl.BlockSpec(memory_space=pltpu.VMEM)
    sem = pltpu.SemaphoreType.DMA
    state = jax.ShapeDtypeStruct(master.shape, F32)
    out = pl.pallas_call(
        kernel,
        out_shape=(state, state, state, jax.ShapeDtypeStruct((8, 8, wide), BF16)),
        in_specs=[any_space] * 7,
        out_specs=(vmem,) * 4,
        scratch_shapes=[
            pltpu.VMEM((tokens, rows), BF16),
            pltpu.VMEM((rows, tokens), BF16),
            pltpu.VMEM((CHUNKS, tokens, 2 * WIDE), BF16),
            pltpu.VMEM((3, 8, wide), F32),
            pltpu.SMEM((1,), jnp.int32),
            pltpu.SMEM((8,), jnp.int32),
            pltpu.VMEM((CHUNKS, 4, 4, 4, 16, WIDE), BF16),
            pltpu.VMEM((CHUNKS, 4, 4, 16, WIDE), BF16),
            pltpu.VMEM((CHUNKS, 4, 16, WIDE), BF16),
            pltpu.VMEM((CHUNKS, 6, 2, 4, 16, WIDE), BF16),
            pltpu.VMEM((CHUNKS, 6, 2, 16, WIDE), BF16),
            pltpu.VMEM((CHUNKS, 3, 16, WIDE), BF16),
            pltpu.VMEM((CHUNKS, 2, 2, 4, 16, WIDE), BF16),
            pltpu.VMEM((CHUNKS, 2, 2, 16, WIDE), BF16),
            pltpu.VMEM((CHUNKS, 1, 16, WIDE), BF16),
            *[pltpu.VMEM((8, 16, WIDE), BF16) for _ in range(CHUNKS)],
            sem((6,)),
            sem((CHUNKS, 2)),
            sem((CHUNKS, 6)),
            sem((CHUNKS, 6)),
            sem((CHUNKS, 6)),
            sem((CHUNKS, 6)),
            sem((CHUNKS, 3)),
            sem((CHUNKS, 3)),
            sem((CHUNKS, 7)),
            sem((CHUNKS, 7)),
        ],
        compiler_params=pltpu.CompilerParams(collective_id=0, has_side_effects=True),
        name="reduce_update_publish",
    )(layer_inputs, cotangent, master, first_moment, second_moment, step_count, owner)
    return out


def solution(mesh):
    split = Mesh(mesh.devices.reshape(4, 4, 4, 4, 2), AXES)
    one = P(GROUP, DP, None)
    return jax.shard_map(
        per_device,
        mesh=split,
        in_specs=(one, one, one, one, one, P(GROUP), P()),
        out_specs=(one, one, one, P(None, DP, None)),
        check_vma=False,
    )
```

```python
import functools
import math

import jax
import jax.numpy as jnp
from jax import lax
from jax.experimental import pallas as pl
from jax.experimental.pallas import tpu as pltpu
from jax.sharding import Mesh
from jax.sharding import PartitionSpec as P

MESH = pl.DeviceIdType.MESH
AXES = ("x", "zh", "y", "zl", "core")
DP = ("x", "zh", "y")
GROUP = ("zl", "core")
HALF = 1024
QUARTER = 512
LIMIT = 24 * 2**20
ORDER = (
    (0, 0), (0, 1), (1, 0), (0, 2), (1, 1), (2, 0), (0, 3), (1, 2),
    (2, 1), (1, 3), (3, 0), (2, 2), (3, 1), (2, 3), (3, 2), (3, 3),
)
F32 = jnp.float32
BF16 = jnp.bfloat16


def kernel(
    x_hbm, ct_hbm, master_hbm, first_hbm, second_hbm, step_s,
    news_out, gathered,
    x_v, xt_v, ct_v, state_v, news_v, pub_v,
    w1, w2, w3, own3, rx1, rx2, rx3, fw1,
    x_sem, ct_sem, state_sem, out_sem, send_sem, relay_sem, finish_sem, last_sem, pub_sem, chip_sem, ready,
):
    x, zh, y = (lax.axis_index(a) for a in DP)
    zl, core = (lax.axis_index(a) for a in GROUP)
    rank = zl * 2 + core

    barrier = pltpu.get_barrier_semaphore()
    near = [{a: lax.rem(i + d, 4)} for a, i in (("x", x), ("y", y)) for d in (1, 2, 3)]

    def signal(sem, device):
        pl.semaphore_signal(sem, inc=1, device_id=device, device_id_type=MESH)

    def signal_along(sem, me, count, place, higher):
        for t in range(count):
            @pl.when((me < t) if higher else (me > t))
            def _():
                signal(sem, place(t))

    def plane(t):
        return {"zh": t}

    def peer(t):
        return {"zl": t // 2, "core": t % 2}

    for device in near:
        signal(barrier, device)
    signal_along(barrier, zh, 4, plane, True)
    signal_along(barrier, rank, 8, peer, True)

    pltpu.make_async_copy(x_hbm.at[0], x_v, x_sem).start()
    for color in range(2):
        for part in range(4):
            cut = pl.ds(part * 192, 192)
            pltpu.make_async_copy(
                ct_hbm.at[0, cut, pl.ds(color * HALF, HALF)], ct_v.at[color, cut], ct_sem.at[color]
            ).start()
    for i, ref in enumerate((master_hbm, first_hbm, second_hbm)):
        pltpu.make_async_copy(ref.at[0], state_v.at[i], state_sem).start()

    def local_wait(ref, sem):
        pltpu.make_async_copy(ref, ref, sem).wait()

    def whole(ref, send, recv):
        return pltpu.make_async_remote_copy(
            src_ref=ref, dst_ref=ref, send_sem=send, recv_sem=recv,
            device_id=near[0], device_id_type=MESH,
        )

    def geometry(stage, c):
        i = (c + stage) % 2
        return ("x", "y")[i], (x, y)[i]

    def halves(c):
        _, pos = geometry(0, c)
        for part, way in ((0, 1), (1, -1)):
            yield (part, pl.ds(2 * part, 2), *(lax.rem(pos + 4 + way * d, 4) for d in (1, -1, 2)))

    def send(c, src, slot, target):
        sem = relay_sem if slot < 2 else finish_sem.at[0]
        pltpu.make_async_remote_copy(
            src_ref=src,
            dst_ref=rx1.at[c, slot],
            send_sem=send_sem.at[0],
            recv_sem=sem.at[c],
            device_id={geometry(0, c)[0]: target},
            device_id_type=MESH,
        ).start()

    def begin(c):
        for part, cut, ahead, _, far in halves(c):
            send(c, w1.at[c, far, cut], part, ahead)
        for part, cut, _, behind, _ in halves(c):
            send(c, w1.at[c, behind, cut], 2 + part, behind)

    def relay(c):
        whole(rx1.at[c, pl.ds(0, 2)], send_sem.at[0], relay_sem.at[c]).wait_recv()
        for part, cut, ahead, _, _ in halves(c):
            total = w1[c, ahead, cut].astype(F32) + rx1[c, part].astype(F32)
            fw1[c, part] = total.astype(BF16)
            send(c, fw1.at[c, part], 4 + part, ahead)

    def spread_rows(c):
        whole(rx1.at[c, pl.ds(2, 4)], send_sem.at[0], finish_sem.at[0, c]).wait_recv()
        _, pos = geometry(0, c)
        for part, cut, _, _, _ in halves(c):
            total = w1[c, pos, cut].astype(F32) + rx1[c, 2 + part].astype(F32)
            w2[c, cut] = (total + rx1[c, 4 + part].astype(F32)).astype(BF16)
        axis, pos = geometry(1, c)
        for d in (2, 1, 3):
            target = lax.rem(pos + d, 4)
            pltpu.make_async_remote_copy(
                src_ref=w2.at[c, target],
                dst_ref=rx2.at[c, 3 - d],
                send_sem=send_sem.at[1],
                recv_sem=finish_sem.at[1, c],
                device_id={axis: target},
                device_id_type=MESH,
            ).start()

    def gather_rows(d, c):
        whole(rx2.at[c], send_sem.at[1], finish_sem.at[1, c]).wait_recv()
        _, pos = geometry(1, c)
        total = w2[c, pos].astype(F32)
        for slot in range(3):
            total = total + rx2[c, slot].astype(F32)
        own3[c] = total
        w3[c] = total.astype(BF16)
        to_owner(d, c)

    def product(d, color):
        c = 2 * d + color
        lhs = xt_v[:, d].reshape(128, xt_v.shape[3])
        res = lax.dot_general(
            lhs, ct_v[color], (((1,), (0,)), ((), ())), preferred_element_type=F32
        )
        res = res.reshape(4, 4, 8, HALF)
        res = jnp.concatenate([res[..., :QUARTER], res[..., QUARTER:]], axis=2).astype(BF16)
        for i in range(4):
            for j in range(4):
                if color == 0:
                    w1[c, i, j] = res[i, j]
                else:
                    w1[c, j, i] = res[i, j]

    def to_owner(d, c):
        if c % 2 == 0 and d > 0:
            @pl.when(zh == d - 1)
            def _():
                pl.semaphore_wait(ready.at[0], 3 - zh)

        @pl.when(zh != d)
        def _():
            slot = lax.rem(zh + 3 - d, 4)
            pltpu.make_async_remote_copy(
                src_ref=w3.at[c],
                dst_ref=rx3.at[c % 2, slot],
                send_sem=send_sem.at[2],
                recv_sem=last_sem.at[c % 2],
                device_id={"zh": d},
                device_id_type=MESH,
            ).start()

    def run(phase, d, color):
        c = 2 * d + color
        if phase == 0:
            product(d, color)
            if c == 0:
                pl.semaphore_wait(barrier, len(near) + zh + rank)
            begin(c)
            if c == 0:
                signal_along(ready.at[0], zh, 4, plane, False)
                signal_along(ready.at[1], rank, 8, peer, False)
        elif phase == 1:
            relay(c)
        elif phase == 2:
            spread_rows(c)
        else:
            gather_rows(d, c)

    def copy_rank(src, color, at, sem, device):
        pltpu.make_async_remote_copy(
            src_ref=src,
            dst_ref=gathered.at[color, at],
            send_sem=send_sem.at[3],
            recv_sem=sem,
            device_id=device,
            device_id_type=MESH,
        ).start()

    def forward(color):
        for d in (1, 2, 3):
            at = lax.rem(zl + 4 - d, 4) * 2 + core
            block = gathered.at[color, at]
            whole(block, send_sem.at[3], chip_sem.at[color, d - 1]).wait_recv()
            copy_rank(block, color, at, pub_sem.at[color], {"core": 1 - core})

    def update(color):
        whole(rx3.at[color], send_sem.at[2], last_sem.at[color]).wait_recv()
        grad = own3[2 * zh + color]
        for slot in range(3):
            grad = grad + rx3[color, slot].astype(F32)
        t = (step_s[0] + 1).astype(F32)
        steps = jnp.full((8, QUARTER), t, F32)
        corr_one = 1.0 - jnp.exp(steps * math.log(0.9))
        corr_two = 1.0 - jnp.exp(steps * math.log(0.999))
        news = []
        for h in range(2):
            cut = pl.ds(color * HALF + h * QUARTER, QUARTER)
            g = grad[8 * h : 8 * h + 8]
            old = state_v[0, :, cut]
            new_first = 0.9 * state_v[1, :, cut] + 0.1 * g
            new_second = 0.999 * state_v[2, :, cut] + 0.001 * g * g
            step = new_first / corr_one / (jnp.sqrt(new_second / corr_two) + 1e-08) + 0.1 * old
            new_master = old - 0.02 * step
            news_v[0, :, cut] = new_master
            news_v[1, :, cut] = new_first
            news_v[2, :, cut] = new_second
            news.append(new_master)
        pub_v[color] = jnp.concatenate(news, axis=0).astype(BF16)
        if color == 0:
            @pl.when(rank < 7)
            def _():
                pl.semaphore_wait(ready.at[1], 7 - rank)

        for d in (1, 2, 3):
            copy_rank(pub_v.at[color], color, rank, chip_sem.at[color, d - 1], {"zl": lax.rem(zl + d, 4)})
        copy_rank(pub_v.at[color], color, rank, pub_sem.at[color], {"core": 1 - core})
        pltpu.make_async_copy(pub_v.at[color], gathered.at[color, rank], out_sem.at[0]).start()

    local_wait(x_v, x_sem)
    xt_v[...] = x_v[...].T.reshape(xt_v.shape)
    for phase, d in ORDER:
        for color in range(2):
            if phase == 0 and d == 0:
                local_wait(ct_v.at[color], ct_sem.at[color])
            run(phase, d, color)
    local_wait(state_v, state_sem)
    for color in range(2):
        update(color)
    pltpu.make_async_copy(news_v, news_out, out_sem.at[1]).start()
    for color in range(2):
        forward(color)

    whole(rx1, send_sem.at[0], send_sem.at[0]).wait_send()
    whole(rx2, send_sem.at[1], send_sem.at[1]).wait_send()
    whole(rx3, send_sem.at[2], send_sem.at[2]).wait_send()
    whole(gathered.at[:, pl.ds(0, 7)], send_sem.at[3], send_sem.at[3]).wait_send()
    local_wait(pub_v, out_sem.at[0])
    local_wait(news_v, out_sem.at[1])
    for color in range(2):
        whole(gathered.at[color, pl.ds(0, 4)], send_sem.at[3], pub_sem.at[color]).wait_recv()


def spread(owner_s, news, gathered, master_out, first_out, second_out, pub_out):
    for i, out in enumerate((master_out, first_out, second_out)):
        out[0] = news[i]
    for b in range(8):
        for color in range(2):
            block = gathered[color, owner_s[b]].astype(F32)
            for h in range(2):
                cut = pl.ds(color * HALF + h * QUARTER, QUARTER)
                pub_out[b, :, cut] = block[8 * h : 8 * h + 8].astype(BF16)


def per_device(layer_inputs, cotangent, master, first_moment, second_moment, step_count, owner):
    tokens, rows = layer_inputs.shape[1:]
    wide = cotangent.shape[2]
    any_space = pl.BlockSpec(memory_space=pl.ANY)
    vmem = pl.BlockSpec(memory_space=pltpu.VMEM)
    smem = pl.BlockSpec(memory_space=pltpu.SMEM)
    sem = pltpu.SemaphoreType.DMA
    state = jax.ShapeDtypeStruct(master.shape, F32)
    held = [
        pltpu.with_memory_space_constraint(a, pltpu.HBM)
        for a in (layer_inputs, cotangent, master, first_moment, second_moment)
    ]
    news, gathered = pl.pallas_call(
        kernel,
        out_shape=(
            jax.ShapeDtypeStruct((3, 8, wide), F32),
            jax.ShapeDtypeStruct((2, 8, 16, QUARTER), BF16),
        ),
        in_specs=[pl.BlockSpec(memory_space=pltpu.HBM)] * 5 + [smem],
        out_specs=(any_space,) * 2,
        scratch_shapes=[
            pltpu.VMEM((tokens, rows), BF16),
            pltpu.VMEM((4, 4, 32, tokens), BF16),
            pltpu.VMEM((2, tokens, HALF), BF16),
            pltpu.VMEM((3, 8, wide), F32),
            pltpu.VMEM((3, 8, wide), F32),
            pltpu.VMEM((2, 16, QUARTER), BF16),
            pltpu.VMEM((8, 4, 4, 16, QUARTER), BF16),
            pltpu.VMEM((8, 4, 16, QUARTER), BF16),
            pltpu.VMEM((8, 16, QUARTER), BF16),
            pltpu.VMEM((8, 16, QUARTER), F32),
            pltpu.VMEM((8, 6, 2, 16, QUARTER), BF16),
            pltpu.VMEM((8, 3, 16, QUARTER), BF16),
            pltpu.VMEM((2, 3, 16, QUARTER), BF16),
            pltpu.VMEM((8, 2, 2, 16, QUARTER), BF16),
            sem,
            sem((2,)),
            sem,
            sem((2,)),
            sem((4,)),
            sem((8,)),
            sem((2, 8)),
            sem((2,)),
            sem((2,)),
            sem((2, 3)),
            pltpu.SemaphoreType.REGULAR((2,)),
        ],
        compiler_params=pltpu.CompilerParams(
            collective_id=0, has_side_effects=True, vmem_limit_bytes=LIMIT
        ),
        name="reduce_update_publish",
    )(*held, step_count)
    return pl.pallas_call(
        spread,
        out_shape=(state, state, state, jax.ShapeDtypeStruct((8, 8, wide), BF16)),
        in_specs=[smem, vmem, vmem],
        out_specs=(vmem,) * 4,
        compiler_params=pltpu.CompilerParams(vmem_limit_bytes=8 * 2**20),
        name="spread",
    )(owner, news, gathered)


def solution(mesh):
    split = Mesh(mesh.devices.reshape(4, 4, 4, 4, 2), AXES)
    one = P(GROUP, DP, None)
    return jax.shard_map(
        per_device,
        mesh=split,
        in_specs=(one, one, one, one, one, P(GROUP), P()),
        out_specs=(one, one, one, P(None, DP, None)),
        check_vma=False,
    )
```

```python
import functools
import math

import jax
import jax.numpy as jnp
from jax import lax
from jax.experimental import pallas as pl
from jax.experimental.pallas import tpu as pltpu
from jax.sharding import Mesh
from jax.sharding import PartitionSpec as P

MESH = pl.DeviceIdType.MESH
AXES = ("x", "zh", "y", "zl", "core")
DP = ("x", "zh", "y")
GROUP = ("zl", "core")
GROUPS = 2
FORWARDED = 1
CHUNKS = 4 * GROUPS
COLS = 2048 // GROUPS
HALF = COLS // 2
LIMIT = 24 * 2**20
ORDER = (
    (0, 0), (0, 1), (1, 0), (0, 2), (1, 1), (2, 0), (1, 2), (0, 3),
    (2, 1), (3, 0), (1, 3), (2, 2), (3, 1), (2, 3), (3, 2), (3, 3),
)
F32 = jnp.float32
BF16 = jnp.bfloat16


def kernel(
    x_hbm, ct_hbm, master_hbm, first_hbm, second_hbm, step_s,
    news_out, gathered,
    x_v, xt_v, ct_v, state_v, news_v, pub_v,
    w1, w2, w3, own3, rx1, rx2, rx3, fw1,
    x_sem, ct_sem, state_sem, out_sem, send_sem, relay_sem, finish_sem, last_sem, pub_sem, chip_sem, ready,
):
    x, zh, y = (lax.axis_index(a) for a in DP)
    zl, core = (lax.axis_index(a) for a in GROUP)
    rank = zl * 2 + core

    def load_columns(g):
        for part in range(2):
            cut = pl.ds(part * 384, 384)
            pltpu.make_async_copy(
                ct_hbm.at[0, cut, pl.ds(g * COLS, COLS)], ct_v.at[g, cut], ct_sem.at[g]
            ).start()

    pltpu.make_async_copy(x_hbm.at[0], x_v, x_sem).start()
    load_columns(0)

    barrier = pltpu.get_barrier_semaphore()
    near = [{a: lax.rem(i + d, 4)} for a, i in (("x", x), ("y", y)) for d in (1, 2, 3)]

    def signal(sem, device):
        pl.semaphore_signal(sem, inc=1, device_id=device, device_id_type=MESH)

    def signal_along(sem, me, count, place, higher):
        for t in range(count):
            @pl.when((me < t) if higher else (me > t))
            def _():
                signal(sem, place(t))

    def plane(t):
        return {"zh": t}

    def peer(t):
        return {"zl": t // 2, "core": t % 2}

    for device in near:
        signal(barrier, device)
    signal_along(barrier, zh, 4, plane, True)
    signal_along(barrier, rank, 8, peer, True)

    for g in range(1, GROUPS):
        load_columns(g)
    for i, ref in enumerate((master_hbm, first_hbm, second_hbm)):
        pltpu.make_async_copy(ref.at[0], state_v.at[i], state_sem).start()

    def local_wait(ref, sem):
        pltpu.make_async_copy(ref, ref, sem).wait()

    def whole(ref, send, recv):
        return pltpu.make_async_remote_copy(
            src_ref=ref, dst_ref=ref, send_sem=send, recv_sem=recv,
            device_id=near[0], device_id_type=MESH,
        )

    def geometry(stage, c):
        i = (c + stage) % 2
        return ("x", "y")[i], (x, y)[i]

    def halves(c):
        _, pos = geometry(0, c)
        for part, way in ((0, 1), (1, -1)):
            yield (part, pl.ds(2 * part, 2), *(lax.rem(pos + 4 + way * d, 4) for d in (1, -1, 2)))

    def send(c, src, slot, target):
        sem = relay_sem if slot < 2 else finish_sem.at[0]
        pltpu.make_async_remote_copy(
            src_ref=src,
            dst_ref=rx1.at[c, slot],
            send_sem=send_sem.at[0],
            recv_sem=sem.at[c],
            device_id={geometry(0, c)[0]: target},
            device_id_type=MESH,
        ).start()

    def begin(c):
        for part, cut, ahead, _, far in halves(c):
            send(c, w1.at[c, far, cut], part, ahead)
        for part, cut, _, behind, _ in halves(c):
            send(c, w1.at[c, behind, cut], 2 + part, behind)

    def relay(c):
        whole(rx1.at[c, pl.ds(0, 2)], send_sem.at[0], relay_sem.at[c]).wait_recv()
        for part, cut, ahead, _, _ in halves(c):
            total = w1[c, ahead, cut].astype(F32) + rx1[c, part].astype(F32)
            fw1[c, part] = total.astype(BF16)
            send(c, fw1.at[c, part], 4 + part, ahead)

    def spread_rows(c):
        whole(rx1.at[c, pl.ds(2, 4)], send_sem.at[0], finish_sem.at[0, c]).wait_recv()
        _, pos = geometry(0, c)
        for part, cut, _, _, _ in halves(c):
            total = w1[c, pos, cut].astype(F32) + rx1[c, 2 + part].astype(F32)
            w2[c, cut] = (total + rx1[c, 4 + part].astype(F32)).astype(BF16)
        axis, pos = geometry(1, c)
        for d in (2, 1, 3):
            target = lax.rem(pos + d, 4)
            pltpu.make_async_remote_copy(
                src_ref=w2.at[c, target],
                dst_ref=rx2.at[c, 3 - d],
                send_sem=send_sem.at[1],
                recv_sem=finish_sem.at[1, c],
                device_id={axis: target},
                device_id_type=MESH,
            ).start()

    def gather_rows(d, c):
        whole(rx2.at[c], send_sem.at[1], finish_sem.at[1, c]).wait_recv()
        _, pos = geometry(1, c)
        total = w2[c, pos].astype(F32)
        for slot in range(3):
            total = total + rx2[c, slot].astype(F32)
        own3[c] = total
        w3[c] = total.astype(BF16)
        to_owner(d, c)

    def product(d, g):
        c = GROUPS * d + g
        lhs = xt_v[:, d].reshape(128, xt_v.shape[3])
        res = lax.dot_general(lhs, ct_v[g], (((1,), (0,)), ((), ())), preferred_element_type=F32)
        res = res.reshape(4, 4, 8, COLS)
        res = jnp.concatenate([res[..., :HALF], res[..., HALF:]], axis=2).astype(BF16)
        for i in range(4):
            for j in range(4):
                if g % 2 == 0:
                    w1[c, i, j] = res[i, j]
                else:
                    w1[c, j, i] = res[i, j]

    def to_owner(d, c):
        if c % GROUPS == 0 and d > 0:
            @pl.when(zh == d - 1)
            def _():
                pl.semaphore_wait(ready.at[0], 3 - zh)

        @pl.when(zh != d)
        def _():
            slot = lax.rem(zh + 3 - d, 4)
            pltpu.make_async_remote_copy(
                src_ref=w3.at[c],
                dst_ref=rx3.at[c % GROUPS, slot],
                send_sem=send_sem.at[2],
                recv_sem=last_sem.at[c % GROUPS],
                device_id={"zh": d},
                device_id_type=MESH,
            ).start()

    def run(phase, c):
        d, g = divmod(c, GROUPS)
        if phase == 0:
            if d == 0:
                local_wait(ct_v.at[g], ct_sem.at[g])
            product(d, g)
            if c == 0:
                pl.semaphore_wait(barrier, len(near) + zh + rank)
            begin(c)
            if c == 3:
                signal_along(ready.at[0], zh, 4, plane, False)
                signal_along(ready.at[1], rank, 8, peer, False)
        elif phase == 1:
            relay(c)
        elif phase == 2:
            spread_rows(c)
        else:
            gather_rows(d, c)

    def copy_rank(src, g, at, sem, device):
        pltpu.make_async_remote_copy(
            src_ref=src,
            dst_ref=gathered.at[at, :, pl.ds(g * COLS, COLS)],
            send_sem=send_sem.at[3],
            recv_sem=sem,
            device_id=device,
            device_id_type=MESH,
        ).start()

    def forward(g):
        for d in (1, 2, 3):
            at = lax.rem(zl + 4 - d, 4) * 2 + core
            block = gathered.at[at, :, pl.ds(g * COLS, COLS)]
            whole(block, send_sem.at[3], chip_sem.at[g, d - 1]).wait_recv()
            copy_rank(block, g, at, pub_sem.at[g], {"core": 1 - core})

    def update(g):
        whole(rx3.at[g], send_sem.at[2], last_sem.at[g]).wait_recv()
        grad = own3[GROUPS * zh + g]
        for slot in range(3):
            grad = grad + rx3[g, slot].astype(F32)
        news = []
        for h in range(2):
            cut = pl.ds(g * COLS + h * HALF, HALF)
            part = grad[8 * h : 8 * h + 8]
            old = state_v[0, :, cut]
            new_first = 0.9 * state_v[1, :, cut] + 0.1 * part
            new_second = 0.999 * state_v[2, :, cut] + 0.001 * part * part
            step = new_first / corr_one / (jnp.sqrt(new_second / corr_two) + 1e-08) + 0.1 * old
            new_master = old - 0.02 * step
            news_v[0, :, cut] = new_master
            news_v[1, :, cut] = new_first
            news_v[2, :, cut] = new_second
            news.append(new_master)
        pub_v[g] = jnp.concatenate(news, axis=1).astype(BF16)
        if g == 0:

            @pl.when(rank < 7)
            def _():
                pl.semaphore_wait(ready.at[1], 7 - rank)

        for k in range(3):
            d = 3 - k + (zl // 2) * (2 * k - 2)
            chip = lax.rem(zl + d, 4)
            if g < FORWARDED:
                copy_rank(pub_v.at[g], g, rank, chip_sem.at[g, d - 1], {"zl": chip})
            else:
                for other in range(2):
                    copy_rank(pub_v.at[g], g, rank, pub_sem.at[g], {"zl": chip, "core": other})
        copy_rank(pub_v.at[g], g, rank, pub_sem.at[g], {"core": 1 - core})
        pltpu.make_async_copy(
            pub_v.at[g], gathered.at[rank, :, pl.ds(g * COLS, COLS)], out_sem.at[0]
        ).start()

    local_wait(x_v, x_sem)
    xt_v[...] = x_v[...].T.reshape(xt_v.shape)
    for phase, pair in ORDER:
        for color in range(2):
            run(phase, 2 * pair + color)
    local_wait(state_v, state_sem)
    steps = jnp.full((8, HALF), (step_s[0] + 1).astype(F32), F32)
    corr_one = 1.0 - jnp.exp(steps * math.log(0.9))
    corr_two = 1.0 - jnp.exp(steps * math.log(0.999))
    for g in range(GROUPS):
        update(g)
    pltpu.make_async_copy(news_v, news_out, out_sem.at[1]).start()
    for g in range(FORWARDED):
        forward(g)

    whole(rx1, send_sem.at[0], send_sem.at[0]).wait_send()
    whole(rx2, send_sem.at[1], send_sem.at[1]).wait_send()
    whole(rx3, send_sem.at[2], send_sem.at[2]).wait_send()
    whole(gathered.at[pl.ds(0, 7)], send_sem.at[3], send_sem.at[3]).wait_send()
    local_wait(pub_v, out_sem.at[0])
    local_wait(news_v, out_sem.at[1])
    for g in range(GROUPS):
        expected = 4 if g < FORWARDED else 7
        block = gathered.at[pl.ds(0, expected), :, pl.ds(g * COLS, COLS)]
        whole(block, send_sem.at[3], pub_sem.at[g]).wait_recv()


def spread(owner_s, news, gathered, master_out, first_out, second_out, pub_out, sems):
    copies = [
        pltpu.make_async_copy(news.at[i], out.at[0], sems.at[i])
        for i, out in enumerate((master_out, first_out, second_out))
    ]
    for b in range(8):
        copies.append(
            pltpu.make_async_copy(gathered.at[owner_s[b]], pub_out.at[b], sems.at[3 + b])
        )
    for copy in copies:
        copy.start()
    for copy in copies:
        copy.wait()


def per_device(layer_inputs, cotangent, master, first_moment, second_moment, step_count, owner):
    tokens, rows = layer_inputs.shape[1:]
    wide = cotangent.shape[2]
    any_space = pl.BlockSpec(memory_space=pl.ANY)
    vmem = pl.BlockSpec(memory_space=pltpu.VMEM)
    smem = pl.BlockSpec(memory_space=pltpu.SMEM)
    sem = pltpu.SemaphoreType.DMA
    state = jax.ShapeDtypeStruct(master.shape, F32)
    held = [
        pltpu.with_memory_space_constraint(a, pltpu.HBM)
        for a in (layer_inputs, cotangent, master, first_moment, second_moment)
    ]
    news, gathered = pl.pallas_call(
        kernel,
        out_shape=(
            jax.ShapeDtypeStruct((3, 8, wide), F32),
            jax.ShapeDtypeStruct((8, 8, wide), BF16),
        ),
        in_specs=[pl.BlockSpec(memory_space=pltpu.HBM)] * 5 + [smem],
        out_specs=(any_space,) * 2,
        scratch_shapes=[
            pltpu.VMEM((tokens, rows), BF16),
            pltpu.VMEM((4, 4, 32, tokens), BF16),
            pltpu.VMEM((GROUPS, tokens, COLS), BF16),
            pltpu.VMEM((3, 8, wide), F32),
            pltpu.VMEM((3, 8, wide), F32),
            pltpu.VMEM((GROUPS, 8, COLS), BF16),
            pltpu.VMEM((CHUNKS, 4, 4, 16, HALF), BF16),
            pltpu.VMEM((CHUNKS, 4, 16, HALF), BF16),
            pltpu.VMEM((CHUNKS, 16, HALF), BF16),
            pltpu.VMEM((CHUNKS, 16, HALF), F32),
            pltpu.VMEM((CHUNKS, 6, 2, 16, HALF), BF16),
            pltpu.VMEM((CHUNKS, 3, 16, HALF), BF16),
            pltpu.VMEM((GROUPS, 3, 16, HALF), BF16),
            pltpu.VMEM((CHUNKS, 2, 2, 16, HALF), BF16),
            sem,
            sem((GROUPS,)),
            sem,
            sem((2,)),
            sem((4,)),
            sem((CHUNKS,)),
            sem((2, CHUNKS)),
            sem((GROUPS,)),
            sem((GROUPS,)),
            sem((GROUPS, 3)),
            pltpu.SemaphoreType.REGULAR((2,)),
        ],
        compiler_params=pltpu.CompilerParams(
            collective_id=0, has_side_effects=True, vmem_limit_bytes=LIMIT
        ),
        name="reduce_update_publish",
    )(*held, step_count)
    return pl.pallas_call(
        spread,
        out_shape=(state, state, state, jax.ShapeDtypeStruct((8, 8, wide), BF16)),
        in_specs=[smem, any_space, any_space],
        out_specs=(any_space,) * 4,
        scratch_shapes=[sem((11,))],
        compiler_params=pltpu.CompilerParams(vmem_limit_bytes=8 * 2**20),
        name="spread",
    )(owner, news, gathered)


def solution(mesh):
    split = Mesh(mesh.devices.reshape(4, 4, 4, 4, 2), AXES)
    one = P(GROUP, DP, None)
    return jax.shard_map(
        per_device,
        mesh=split,
        in_specs=(one, one, one, one, one, P(GROUP), P()),
        out_specs=(one, one, one, P(None, DP, None)),
        check_vma=False,
    )
```

```python
import functools
import math

import jax
import jax.numpy as jnp
from jax import lax
from jax.experimental import pallas as pl
from jax.experimental.pallas import tpu as pltpu
from jax.sharding import Mesh
from jax.sharding import PartitionSpec as P

MESH = pl.DeviceIdType.MESH
AXES = ("x", "zh", "y", "zl", "core")
DP = ("x", "zh", "y")
GROUP = ("zl", "core")
GROUPS = 2
FORWARDED = 1
CHUNKS = 4 * GROUPS
COLS = 2048 // GROUPS
HALF = COLS // 2
LIMIT = 24 * 2**20
ORDER = (
    (0, 0), (0, 1), (1, 0), (0, 2), (1, 1), (2, 0), (1, 2), (2, 1),
    (0, 3), (3, 0), (2, 2), (1, 3), (3, 1), (3, 2), (2, 3), (3, 3),
)
F32 = jnp.float32
BF16 = jnp.bfloat16


def kernel(
    x_hbm, ct_hbm, master_hbm, first_hbm, second_hbm, step_s,
    news_out, gathered,
    x_v, xt_v, ct_v, state_v, news_v, pub_v,
    w1, w2, w3, own3, rx1, rx2, rx3, fw1,
    x_sem, ct_sem, state_sem, out_sem, send_sem, relay_sem, finish_sem, last_sem, pub_sem, chip_sem, ready,
):
    x, zh, y = (lax.axis_index(a) for a in DP)
    zl, core = (lax.axis_index(a) for a in GROUP)
    rank = zl * 2 + core

    def load_columns(g):
        for part in range(2):
            cut = pl.ds(part * 384, 384)
            pltpu.make_async_copy(
                ct_hbm.at[0, cut, pl.ds(g * COLS, COLS)], ct_v.at[g, cut], ct_sem.at[g]
            ).start()

    pltpu.make_async_copy(x_hbm.at[0], x_v, x_sem).start()
    load_columns(0)

    barrier = pltpu.get_barrier_semaphore()
    near = [{a: lax.rem(i + d, 4)} for a, i in (("x", x), ("y", y)) for d in (1, 2, 3)]

    def signal(sem, device):
        pl.semaphore_signal(sem, inc=1, device_id=device, device_id_type=MESH)

    def signal_along(sem, me, count, place, higher):
        for t in range(count):
            @pl.when((me < t) if higher else (me > t))
            def _():
                signal(sem, place(t))

    def plane(t):
        return {"zh": t}

    def peer(t):
        return {"zl": t // 2, "core": t % 2}

    for device in near:
        signal(barrier, device)
    signal_along(barrier, zh, 4, plane, True)
    signal_along(barrier, rank, 8, peer, True)

    for g in range(1, GROUPS):
        load_columns(g)
    for i, ref in enumerate((master_hbm, first_hbm, second_hbm)):
        pltpu.make_async_copy(ref.at[0], state_v.at[i], state_sem).start()

    def local_wait(ref, sem):
        pltpu.make_async_copy(ref, ref, sem).wait()

    def whole(ref, send, recv):
        return pltpu.make_async_remote_copy(
            src_ref=ref, dst_ref=ref, send_sem=send, recv_sem=recv,
            device_id=near[0], device_id_type=MESH,
        )

    def geometry(stage, c):
        i = (c + stage) % 2
        return ("x", "y")[i], (x, y)[i]

    def halves(c):
        _, pos = geometry(0, c)
        for part, way in ((0, 1), (1, -1)):
            yield (part, pl.ds(2 * part, 2), *(lax.rem(pos + 4 + way * d, 4) for d in (1, -1, 2)))

    def send(c, src, slot, target):
        sem = relay_sem if slot < 2 else finish_sem.at[0]
        pltpu.make_async_remote_copy(
            src_ref=src,
            dst_ref=rx1.at[c, slot],
            send_sem=send_sem.at[0],
            recv_sem=sem.at[c],
            device_id={geometry(0, c)[0]: target},
            device_id_type=MESH,
        ).start()

    def begin(c):
        for part, cut, ahead, _, far in halves(c):
            send(c, w1.at[c, far, cut], part, ahead)
        for part, cut, _, behind, _ in halves(c):
            send(c, w1.at[c, behind, cut], 2 + part, behind)

    def relay(c):
        whole(rx1.at[c, pl.ds(0, 2)], send_sem.at[0], relay_sem.at[c]).wait_recv()
        for part, cut, ahead, _, _ in halves(c):
            total = w1[c, ahead, cut].astype(F32) + rx1[c, part].astype(F32)
            fw1[c, part] = total.astype(BF16)
            send(c, fw1.at[c, part], 4 + part, ahead)

    def spread_rows(c):
        whole(rx1.at[c, pl.ds(2, 4)], send_sem.at[0], finish_sem.at[0, c]).wait_recv()
        _, pos = geometry(0, c)
        for part, cut, _, _, _ in halves(c):
            total = w1[c, pos, cut].astype(F32) + rx1[c, 2 + part].astype(F32)
            w2[c, cut] = (total + rx1[c, 4 + part].astype(F32)).astype(BF16)
        axis, pos = geometry(1, c)
        for d in (2, 1, 3):
            target = lax.rem(pos + d, 4)
            pltpu.make_async_remote_copy(
                src_ref=w2.at[c, target],
                dst_ref=rx2.at[c, 3 - d],
                send_sem=send_sem.at[1],
                recv_sem=finish_sem.at[1, c],
                device_id={axis: target},
                device_id_type=MESH,
            ).start()

    def gather_rows(d, c):
        whole(rx2.at[c], send_sem.at[1], finish_sem.at[1, c]).wait_recv()
        _, pos = geometry(1, c)
        total = w2[c, pos].astype(F32)
        for slot in range(3):
            total = total + rx2[c, slot].astype(F32)
        own3[c] = total
        w3[c] = total.astype(BF16)
        to_owner(d, c)

    def product(d, g):
        c = GROUPS * d + g
        lhs = xt_v[:, d].reshape(128, xt_v.shape[3])
        res = lax.dot_general(lhs, ct_v[g], (((1,), (0,)), ((), ())), preferred_element_type=F32)
        res = res.reshape(4, 4, 8, COLS)
        res = jnp.concatenate([res[..., :HALF], res[..., HALF:]], axis=2).astype(BF16)
        for i in range(4):
            for j in range(4):
                if g % 2 == 0:
                    w1[c, i, j] = res[i, j]
                else:
                    w1[c, j, i] = res[i, j]

    def to_owner(d, c):
        if c % GROUPS == 0 and d > 0:
            @pl.when(zh == d - 1)
            def _():
                pl.semaphore_wait(ready.at[0], 3 - zh)

        @pl.when(zh != d)
        def _():
            slot = lax.rem(zh + 3 - d, 4)
            pltpu.make_async_remote_copy(
                src_ref=w3.at[c],
                dst_ref=rx3.at[c % GROUPS, slot],
                send_sem=send_sem.at[2],
                recv_sem=last_sem.at[c % GROUPS],
                device_id={"zh": d},
                device_id_type=MESH,
            ).start()

    def run(phase, c):
        d, g = divmod(c, GROUPS)
        if phase == 0:
            if d == 0:
                local_wait(ct_v.at[g], ct_sem.at[g])
            product(d, g)
            if c == 0:
                pl.semaphore_wait(barrier, len(near) + zh + rank)
            begin(c)
            if c == 3:
                signal_along(ready.at[0], zh, 4, plane, False)
                signal_along(ready.at[1], rank, 8, peer, False)
        elif phase == 1:
            relay(c)
        elif phase == 2:
            spread_rows(c)
        else:
            gather_rows(d, c)

    def copy_rank(src, g, at, sem, device):
        pltpu.make_async_remote_copy(
            src_ref=src,
            dst_ref=gathered.at[at, :, pl.ds(g * COLS, COLS)],
            send_sem=send_sem.at[3],
            recv_sem=sem,
            device_id=device,
            device_id_type=MESH,
        ).start()

    def forward(g):
        for d in (1, 2, 3):
            at = lax.rem(zl + 4 - d, 4) * 2 + core
            block = gathered.at[at, :, pl.ds(g * COLS, COLS)]
            whole(block, send_sem.at[3], chip_sem.at[g, d - 1]).wait_recv()
            copy_rank(block, g, at, pub_sem.at[g], {"core": 1 - core})

    def update(g):
        whole(rx3.at[g], send_sem.at[2], last_sem.at[g]).wait_recv()
        grad = own3[GROUPS * zh + g]
        for slot in range(3):
            grad = grad + rx3[g, slot].astype(F32)
        news = []
        for h in range(2):
            cut = pl.ds(g * COLS + h * HALF, HALF)
            part = grad[8 * h : 8 * h + 8]
            old = state_v[0, :, cut]
            new_first = 0.9 * state_v[1, :, cut] + 0.1 * part
            new_second = 0.999 * state_v[2, :, cut] + 0.001 * part * part
            step = new_first / corr_one / (jnp.sqrt(new_second / corr_two) + 1e-08) + 0.1 * old
            new_master = old - 0.02 * step
            news_v[0, :, cut] = new_master
            news_v[1, :, cut] = new_first
            news_v[2, :, cut] = new_second
            news.append(new_master)
        pub_v[g] = jnp.concatenate(news, axis=1).astype(BF16)
        if g == 0:

            @pl.when(rank < 7)
            def _():
                pl.semaphore_wait(ready.at[1], 7 - rank)

        for k in range(3):
            d = 3 - k + (zl // 2) * (2 * k - 2)
            chip = lax.rem(zl + d, 4)
            if g < FORWARDED:
                copy_rank(pub_v.at[g], g, rank, chip_sem.at[g, d - 1], {"zl": chip})
            else:
                for other in range(2):
                    copy_rank(pub_v.at[g], g, rank, pub_sem.at[g], {"zl": chip, "core": other})
        copy_rank(pub_v.at[g], g, rank, pub_sem.at[g], {"core": 1 - core})
        pltpu.make_async_copy(
            pub_v.at[g], gathered.at[rank, :, pl.ds(g * COLS, COLS)], out_sem.at[0]
        ).start()

    local_wait(x_v, x_sem)
    xt_v[...] = x_v[...].T.reshape(xt_v.shape)
    for phase, pair in ORDER:
        for color in range(2):
            run(phase, 2 * pair + color)
    local_wait(state_v, state_sem)
    steps = jnp.full((8, HALF), (step_s[0] + 1).astype(F32), F32)
    corr_one = 1.0 - jnp.exp(steps * math.log(0.9))
    corr_two = 1.0 - jnp.exp(steps * math.log(0.999))
    for g in range(GROUPS):
        update(g)
    pltpu.make_async_copy(news_v, news_out, out_sem.at[1]).start()
    for g in range(FORWARDED):
        forward(g)

    whole(rx1, send_sem.at[0], send_sem.at[0]).wait_send()
    whole(rx2, send_sem.at[1], send_sem.at[1]).wait_send()
    whole(rx3, send_sem.at[2], send_sem.at[2]).wait_send()
    whole(gathered.at[pl.ds(0, 7)], send_sem.at[3], send_sem.at[3]).wait_send()
    local_wait(pub_v, out_sem.at[0])
    local_wait(news_v, out_sem.at[1])
    for g in range(GROUPS):
        expected = 4 if g < FORWARDED else 7
        block = gathered.at[pl.ds(0, expected), :, pl.ds(g * COLS, COLS)]
        whole(block, send_sem.at[3], pub_sem.at[g]).wait_recv()


def spread(owner_s, news, gathered, master_out, first_out, second_out, pub_out, sems):
    copies = [
        pltpu.make_async_copy(news.at[i], out.at[0], sems.at[i])
        for i, out in enumerate((master_out, first_out, second_out))
    ]
    for b in range(8):
        copies.append(
            pltpu.make_async_copy(gathered.at[owner_s[b]], pub_out.at[b], sems.at[3 + b])
        )
    for copy in copies:
        copy.start()
    for copy in copies:
        copy.wait()


def per_device(layer_inputs, cotangent, master, first_moment, second_moment, step_count, owner):
    tokens, rows = layer_inputs.shape[1:]
    wide = cotangent.shape[2]
    any_space = pl.BlockSpec(memory_space=pl.ANY)
    vmem = pl.BlockSpec(memory_space=pltpu.VMEM)
    smem = pl.BlockSpec(memory_space=pltpu.SMEM)
    sem = pltpu.SemaphoreType.DMA
    state = jax.ShapeDtypeStruct(master.shape, F32)
    held = [
        pltpu.with_memory_space_constraint(a, pltpu.HBM)
        for a in (layer_inputs, cotangent, master, first_moment, second_moment)
    ]
    news, gathered = pl.pallas_call(
        kernel,
        out_shape=(
            jax.ShapeDtypeStruct((3, 8, wide), F32),
            jax.ShapeDtypeStruct((8, 8, wide), BF16),
        ),
        in_specs=[pl.BlockSpec(memory_space=pltpu.HBM)] * 5 + [smem],
        out_specs=(any_space,) * 2,
        scratch_shapes=[
            pltpu.VMEM((tokens, rows), BF16),
            pltpu.VMEM((4, 4, 32, tokens), BF16),
            pltpu.VMEM((GROUPS, tokens, COLS), BF16),
            pltpu.VMEM((3, 8, wide), F32),
            pltpu.VMEM((3, 8, wide), F32),
            pltpu.VMEM((GROUPS, 8, COLS), BF16),
            pltpu.VMEM((CHUNKS, 4, 4, 16, HALF), BF16),
            pltpu.VMEM((CHUNKS, 4, 16, HALF), BF16),
            pltpu.VMEM((CHUNKS, 16, HALF), BF16),
            pltpu.VMEM((CHUNKS, 16, HALF), F32),
            pltpu.VMEM((CHUNKS, 6, 2, 16, HALF), BF16),
            pltpu.VMEM((CHUNKS, 3, 16, HALF), BF16),
            pltpu.VMEM((GROUPS, 3, 16, HALF), BF16),
            pltpu.VMEM((CHUNKS, 2, 2, 16, HALF), BF16),
            sem,
            sem((GROUPS,)),
            sem,
            sem((2,)),
            sem((4,)),
            sem((CHUNKS,)),
            sem((2, CHUNKS)),
            sem((GROUPS,)),
            sem((GROUPS,)),
            sem((GROUPS, 3)),
            pltpu.SemaphoreType.REGULAR((2,)),
        ],
        compiler_params=pltpu.CompilerParams(
            collective_id=0, has_side_effects=True, vmem_limit_bytes=LIMIT
        ),
        name="reduce_update_publish",
    )(*held, step_count)
    return pl.pallas_call(
        spread,
        out_shape=(state, state, state, jax.ShapeDtypeStruct((8, 8, wide), BF16)),
        in_specs=[smem, any_space, any_space],
        out_specs=(any_space,) * 4,
        scratch_shapes=[sem((11,))],
        compiler_params=pltpu.CompilerParams(vmem_limit_bytes=8 * 2**20),
        name="spread",
    )(owner, news, gathered)


def solution(mesh):
    split = Mesh(mesh.devices.reshape(4, 4, 4, 4, 2), AXES)
    one = P(GROUP, DP, None)
    return jax.shard_map(
        per_device,
        mesh=split,
        in_specs=(one, one, one, one, one, P(GROUP), P()),
        out_specs=(one, one, one, P(None, DP, None)),
        check_vma=False,
    )
```
